32 devices in a mesh: group: 2 (over y), seq: 16 (over z, x, core).
Axes of the slice: x: 2, y: 2, z: 4, core: 2. Of those that a mesh axis runs over, the one named last changes fastest.
Arguments:
- inputs: bfloat16 [12544, 1024], P(('group', 'seq')), parts along dimension 0, may hold values from -6 to 6
- out_grad: bfloat16 [12544, 1024], P(('group', 'seq')), parts along dimension 0, may hold values from -6 to 6
- live_rows: int32 [256], P('group'), parts along dimension 0, may hold values from 1 to 7
- live_cols: int32 [256], P('group'), parts along dimension 0, may hold values from 1 to 7
- norm_gain: float32 [1024], replicated, may hold values from 0.25 to 1.75
- norm_bias: float32 [1024], replicated, may hold values from -3 to 3
- w_query: bfloat16 [1024, 1024], replicated
- w_key_value: bfloat16 [1024, 2048], replicated
- w_out: bfloat16 [1024, 1024], replicated, may hold values from -0.1875 to 0.1875
Outputs:
- block_output: bfloat16 [12544, 1024], P(('group', 'seq')), parts along dimension 0
- input_grad: bfloat16 [12544, 1024], P(('group', 'seq')), parts along dimension 0
The draws below stay inside these ranges and needn't reach their ends.
There are 2 independent parts, one for each index of `group`. The reference program is written for one: setup_inputs(seed, part) draws one part's arguments, and reference() takes and returns one part's arrays. A program takes and returns all parts, laid end to end along the dimension named above; an argument that names none is the same for every part. Nothing has to cross between parts.
All inputs are finite; a program needn't handle non-finite values.
Results may differ from the reference program's by a relative error of at most 0.006.
The reference program's roundings to bfloat16 on the way count: a program that leaves them out, or rounds other values in their place, can miss the bound.
Values may be sent and summed in bfloat16 or wider, within the bound.
No kernel may reach another device: no remote copies, remote signals or barrier semaphores. Data moves between devices by JAX's collectives and lax.ppermute only.
A program may use at most 192 MiB of HBM per device.

```python
import math
import jax
import jax.numpy as jnp
from jax import lax

D = 1024
HEAD_DIM = 32
WT = 8
WH = 7
WW = 7
INNER = 1024
CELLS = 49
FRAMES = 128
TOKENS = 6272


def drawn_part(key, salt_value):
    own_part = jax.random.normal(jax.random.fold_in(key, salt_value), (D, INNER), jnp.float32) / math.sqrt(D)
    return own_part


def draw_w_query(key, part):
    return drawn_part(key, 41).astype(jnp.bfloat16)


def draw_w_key_value(key, part):
    value_part = jax.random.normal(jax.random.fold_in(key, 47), (D, INNER), jnp.float32) / math.sqrt(D)
    return jnp.concatenate([drawn_part(key, 43), value_part], axis=1).astype(jnp.bfloat16)


def with_ends(values, rng, least, largest):
    spot = [jax.random.randint(jax.random.fold_in(rng, axis), (), 0, length) for axis, length in enumerate(values.shape)]
    widest = values.shape.index(max(values.shape))
    beside = spot[:widest] + [(spot[widest] + 1) % values.shape[widest]] + spot[widest + 1:]
    return values.at[tuple(spot)].set(least).at[tuple(beside)].set(largest)


def shard_levels(own_key, extent, split, smallest, high):
    level, own = 1.0, jax.random.fold_in(own_key, 6)
    for dim, blocks in split:
        draws = jnp.exp(jax.random.uniform(jax.random.fold_in(own, dim), (blocks,), jnp.float32, smallest / len(split), high / len(split)))
        level = level * jnp.repeat(draws, extent[dim] // blocks).reshape([-1 if axis == dim else 1 for axis in range(len(extent))])
    return level


def bell_draw(stream_key, dims, spread, limit, cuts=(), kind=jnp.bfloat16):
    factor_of = shard_levels(stream_key, dims, cuts, -0.22, 0.18) if cuts else 1.0
    array = jax.random.normal(stream_key, dims, jnp.float32) * spread * factor_of
    return jnp.minimum(jnp.maximum(array, -limit), limit).astype(kind)


def setup_inputs(seed: int = 0, part: int = 0) -> dict:
    splits = jax.random.split(jax.random.key(seed), 10)
    part_splits = jax.random.split(jax.random.fold_in(splits[9], part), 10)
    inputs = bell_draw(part_splits[0], (TOKENS, D), 1.0, 6.0, ((0, 16),))
    out_grad = bell_draw(part_splits[1], (TOKENS, D), 1.0, 6.0, ((0, 16),))
    live_rows = with_ends(jax.random.randint(part_splits[2], (FRAMES,), 1, WH + 1), jax.random.fold_in(part_splits[2], 1), 1, WH).astype(jnp.int32)
    live_cols = with_ends(jax.random.randint(part_splits[3], (FRAMES,), 1, WW + 1), jax.random.fold_in(part_splits[3], 1), 1, WW).astype(jnp.int32)
    norm_gain = jnp.clip(1.0 + 0.15 * jax.random.normal(splits[4], (D,), jnp.float32), 0.25, 1.75)
    norm_bias = bell_draw(splits[5], (D,), 0.5, 3.0, (), jnp.float32)
    w_query = draw_w_query(jax.random.fold_in(splits[9], 71), part)
    w_key_value = draw_w_key_value(jax.random.fold_in(splits[9], 71), part)
    w_out = bell_draw(splits[8], (INNER, D), INNER ** -0.5, 0.1875)
    return dict(inputs=inputs, out_grad=out_grad, live_rows=live_rows, live_cols=live_cols, norm_gain=norm_gain, norm_bias=norm_bias, w_query=w_query, w_key_value=w_key_value, w_out=w_out)


epsilon = 1e-05

def normalize(values_in, norm_gain, norm_bias):
    values = values_in.astype(jnp.float32)
    centred = values - lax.optimization_barrier(jnp.mean(values, axis=-1, keepdims=True))
    inv_dev = lax.rsqrt(lax.optimization_barrier(jnp.mean(centred * centred, axis=-1, keepdims=True)) + epsilon)
    unit_norm = centred * inv_dev
    return ((unit_norm * norm_gain + norm_bias).astype(jnp.bfloat16), unit_norm, inv_dev)

def norm_backward(grad_hidden, unit_norm, inv_dev, norm_gain):
    scaled = grad_hidden * norm_gain
    centred = scaled - lax.optimization_barrier(jnp.mean(scaled, axis=-1, keepdims=True))
    return inv_dev * (centred - unit_norm * lax.optimization_barrier(jnp.mean(scaled * unit_norm, axis=-1, keepdims=True)))

def cell_codes(frame_ids, row_limit, col_limit):
    cell_index = jnp.arange(WH * WW, dtype=jnp.int32)
    cell_row = cell_index // WW
    cell_col = cell_index % WW
    spatial = 2 * (cell_row < WH // 2).astype(jnp.int32) + (cell_col < WW // 2).astype(jnp.int32)
    early_frame = (frame_ids < WT // 2).astype(jnp.int32)
    region = spatial[None, :] + 4 * early_frame[:, None]
    is_live = (cell_row[None, :] < row_limit[:, None]) & (cell_col[None, :] < col_limit[:, None])
    return (region.reshape(-1), is_live.reshape(-1))

def rounded(values):
    return lax.optimization_barrier(values.astype(jnp.bfloat16)).astype(jnp.float32)

def window_attention(window_items):
    queries, key_pair, grad_ctx, query_region, query_live, query_pos, key_region, key_live = window_items
    query_count = queries.shape[0]
    key_count = key_pair.shape[0]
    inner_width = queries.shape[1]
    head_count = inner_width // HEAD_DIM
    score_scale = HEAD_DIM ** (-0.5)
    query_heads = queries.astype(jnp.float32).reshape(query_count, head_count, HEAD_DIM)
    key_heads = key_pair[:, :inner_width].astype(jnp.float32).reshape(key_count, head_count, HEAD_DIM)
    value_heads = key_pair[:, inner_width:].astype(jnp.float32).reshape(key_count, head_count, HEAD_DIM)
    grad_heads = grad_ctx.astype(jnp.float32).reshape(query_count, head_count, HEAD_DIM)
    same_region = (query_region[:, None] == key_region[None, :]) & query_live[:, None] & key_live[None, :]
    allowed = same_region | (query_pos[:, None] == jnp.arange(key_count, dtype=jnp.int32)[None, :])
    scores = jnp.einsum('qhd,khd->hqk', query_heads, key_heads) * score_scale
    scores = jnp.where(allowed[None], scores, -1e+30)
    weights_raw = jnp.exp(scores - lax.optimization_barrier(jnp.max(scores, axis=-1, keepdims=True)))
    soft_probs = weights_raw / lax.optimization_barrier(jnp.sum(weights_raw, axis=-1, keepdims=True))
    probs_low = rounded(soft_probs)
    context = jnp.einsum('hqk,khd->qhd', probs_low, value_heads).astype(jnp.bfloat16).reshape(query_count, inner_width)
    grad_probs = jnp.einsum('qhd,khd->hqk', grad_heads, value_heads)
    grad_value = jnp.einsum('hqk,qhd->khd', probs_low, grad_heads)
    row_dot = lax.optimization_barrier(jnp.sum(soft_probs * grad_probs, axis=-1, keepdims=True))
    grad_scores = rounded(soft_probs * (grad_probs - row_dot) * score_scale)
    grad_query = jnp.einsum('hqk,khd->qhd', grad_scores, key_heads).reshape(query_count, inner_width)
    grad_key = jnp.einsum('hqk,qhd->khd', grad_scores, query_heads).reshape(key_count, inner_width)
    grad_pair = jnp.concatenate([grad_key, grad_value.reshape(key_count, inner_width)], axis=-1)
    return (context, grad_query, grad_pair)

def reference(inputs, out_grad, live_rows, live_cols, norm_gain, norm_bias, w_query, w_key_value, w_out):
    token_total = inputs.shape[0]
    frame_total = token_total // CELLS
    shift_cells = WT // 2 * CELLS
    span = WT * CELLS
    hidden, unit_norm, inv_dev = normalize(inputs, norm_gain, norm_bias)
    queries = jnp.dot(hidden, w_query, preferred_element_type=jnp.float32).astype(jnp.bfloat16)
    key_pair = jnp.dot(hidden, w_key_value, preferred_element_type=jnp.float32).astype(jnp.bfloat16)
    grad_ctx = jnp.dot(out_grad, w_out.T, preferred_element_type=jnp.float32).astype(jnp.bfloat16)
    frame_ids = jnp.arange(frame_total, dtype=jnp.int32)
    region, is_live = cell_codes(frame_ids, live_rows, live_cols)

    def to_windows(values):
        rolled_values = jnp.roll(values, -shift_cells, axis=0)
        return rolled_values.reshape((token_total // span, span) + values.shape[1:])

    def from_windows(values):
        return jnp.roll(values.reshape((token_total,) + values.shape[2:]), shift_cells, axis=0)
    win_region = to_windows(region)
    win_live = to_windows(is_live)
    win_pos = jnp.broadcast_to(jnp.arange(span, dtype=jnp.int32)[None, :], win_region.shape)
    context, grad_query, grad_pair = lax.map(window_attention, (to_windows(queries), to_windows(key_pair), to_windows(grad_ctx), win_region, win_live, win_pos, win_region, win_live))
    context = from_windows(context)
    grad_query = from_windows(grad_query).astype(jnp.bfloat16)
    grad_pair = from_windows(grad_pair).astype(jnp.bfloat16)
    block_output = (inputs.astype(jnp.float32) + jnp.dot(context, w_out, preferred_element_type=jnp.float32)).astype(jnp.bfloat16)
    grad_hidden = jnp.dot(grad_query, w_query.T, preferred_element_type=jnp.float32) + jnp.dot(grad_pair, w_key_value.T, preferred_element_type=jnp.float32)
    input_grad = (out_grad.astype(jnp.float32) + norm_backward(grad_hidden, unit_norm, inv_dev, norm_gain)).astype(jnp.bfloat16)
    return (block_output, input_grad)
```

```python
import functools

import jax
import jax.numpy as jnp
import numpy as np
from jax import lax
from jax.experimental import pallas as pl
from jax.experimental.pallas import tpu as pltpu
from jax.sharding import PartitionSpec as P

HEAD_DIM = 32
WT = 8
WH = 7
WW = 7
CELLS = WH * WW
HALF = WT // 2
EPSILON = 1e-05
GROUP_LANES = 128
HEADS_PER_GROUP = GROUP_LANES // HEAD_DIM
SLOTS = (64, 48)
ROWS = sum(SLOTS)
FIRST = 2 * SLOTS[0]
SECOND = 2 * SLOTS[1]
WINDOW_ROWS = FIRST + SECOND
PADDED_ROWS = 2 * GROUP_LANES
MASKED = -1e30
BF16 = jnp.bfloat16
F32 = jnp.float32
NT = (((1,), (1,)), ((), ()))


def quadrant_cells(quadrant):
    rows = range(WH // 2) if quadrant & 2 else range(WH // 2, WH)
    cols = range(WW // 2) if quadrant & 1 else range(WW // 2, WW)
    return [(row, col) for row in rows for col in cols]


def half_slots(units):
    slots = []
    for quadrant, room in zip(units, SLOTS):
        entries = [(frame, row, col) for frame in range(HALF) for row, col in quadrant_cells(quadrant)]
        slots += entries + [None] * (room - len(entries))
    return slots


def tables():
    takes = {"last": (0, 3), "first": (1, 2)}
    gives = {"last": (1, 2), "first": (0, 3)}

    def tokens(side, units):
        shift = HALF if side == "last" else 0
        return [-1 if s is None else (s[0] + shift) * CELLS + s[1] * WW + s[2] for s in half_slots(units)]

    def codes(slots, second_half):
        return [-1 if s is None else (s[0] + HALF * second_half) * 64 + s[1] * 8 + s[2] for s in slots]

    own, send, window = [], [], []
    for parity in range(2):
        sides = ("last", "first") if parity == 0 else ("first", "last")
        own.append(sum((tokens(side, takes[side]) for side in sides), []))
        send.append(sum((tokens(side, gives[side]) for side in sides), []))
    for side in ("first", "last"):
        slots = half_slots(takes[side])
        mine = codes(slots, side == "first")
        theirs = codes(slots, side == "last")
        cut = SLOTS[0]
        rows = mine[:cut] + theirs[:cut] + mine[cut:] + theirs[cut:]
        window.append(rows + [-1] * (PADDED_ROWS - len(rows)))
    return np.array(own, np.int32), np.array(send, np.int32), np.array(window, np.int32)


OWN_TOKENS, SEND_TOKENS, WINDOW_CODES = tables()


def normalized(values_in):
    values = values_in.astype(F32)
    centred = values - jnp.mean(values, axis=-1, keepdims=True)
    inv_dev = lax.rsqrt(jnp.mean(centred * centred, axis=-1, keepdims=True) + EPSILON)
    return centred * inv_dev, inv_dev


def one_hot_rows(token_column, token_count):
    lanes = lax.broadcasted_iota(jnp.int32, (token_column.shape[0], token_count), 1)
    return (lanes == token_column).astype(F32).astype(BF16)


def picked(one_hot, values):
    return jnp.dot(one_hot, values, preferred_element_type=F32).astype(BF16)


def pack_kernel(meta, table, inputs, out_grad, same, cross):
    width = inputs.shape[1]
    one_hot = one_hot_rows(table[meta[0]], inputs.shape[0])
    for place, source in enumerate((inputs, out_grad)):
        rows = picked(one_hot, source[...])
        columns = slice(place * width, (place + 1) * width)
        same[:, columns] = rows[:ROWS]
        cross[:, columns] = rows[ROWS:]


def project(values, grads, gain, bias, w_query, w_key_value, w_out, store):
    width = values.shape[1]
    unit, _ = normalized(values)
    hidden = (unit * gain[...] + bias[...]).astype(BF16)
    store(0, jnp.dot(hidden, w_query[...], preferred_element_type=F32).astype(BF16))
    store(width, jnp.dot(hidden, w_key_value[...], preferred_element_type=F32).astype(BF16))
    store(3 * width, lax.dot_general(grads, w_out[...], NT, preferred_element_type=F32).astype(BF16))


def own_kernel(
    meta, table, inputs, out_grad, gain, bias, w_query, w_key_value, w_out, rows_same, rows_cross, heads_same, heads_cross
):
    width = inputs.shape[1]
    one_hot = one_hot_rows(table[meta[0]], inputs.shape[0])
    values = picked(one_hot, inputs[...])
    grads = picked(one_hot, out_grad[...])
    for place, rows in enumerate((values, grads)):
        columns = slice(place * width, (place + 1) * width)
        rows_same[:, columns] = rows[:ROWS]
        rows_cross[:, columns] = rows[ROWS:]

    def store(column, result):
        columns = slice(column, column + result.shape[1])
        heads_same[:, columns] = result[:ROWS]
        heads_cross[:, columns] = result[ROWS:]

    project(values, grads, gain, bias, w_query, w_key_value, w_out, store)


def cell_codes(slots, place, frames):
    frame = slots >> 6
    word = jnp.zeros_like(slots)
    for index, frame_word in enumerate(frames):
        word = jnp.where(frame == index, frame_word, word)
    row, col = (slots >> 3) & 7, slots & 7
    live = (slots >= 0) & (row < (word >> 8)) & (col < ((word >> 4) & 15))
    return jnp.where(live, word & 1, -1 - place)


def attend(heads, results, bias_of, group, width):
    scale = HEAD_DIM ** (-0.5)
    lane = lax.broadcasted_iota(jnp.int32, (GROUP_LANES, GROUP_LANES), 1) // HEAD_DIM

    def columns(part):
        return pl.ds(pl.multiple_of(part * width + group * GROUP_LANES, GROUP_LANES), GROUP_LANES)

    for unit, count in enumerate((FIRST, SECOND)):
        base = unit * GROUP_LANES
        keys = slice(base, base + count)
        query = heads[base : base + GROUP_LANES, columns(0)]
        key = heads[keys, columns(1)]
        value = heads[keys, columns(2)]
        grad = heads[base : base + GROUP_LANES, columns(3)]
        zero = jnp.zeros_like(query)
        query_stack = jnp.concatenate([jnp.where(lane == h, query, zero) for h in range(HEADS_PER_GROUP)], axis=0)
        grad_stack = jnp.concatenate([jnp.where(lane == h, grad, zero) for h in range(HEADS_PER_GROUP)], axis=0)
        score = lax.dot_general(key, query_stack, NT, preferred_element_type=F32)
        grad_probs = lax.dot_general(value, grad_stack, NT, preferred_element_type=F32)
        bias = bias_of[keys, :]
        bias = jnp.concatenate([bias] * HEADS_PER_GROUP, axis=1)
        score = score * scale + bias
        raw = jnp.exp(score - jnp.max(score, axis=0, keepdims=True))
        probs = raw * (1.0 / jnp.sum(raw, axis=0, keepdims=True))
        row_dot = jnp.sum(probs * grad_probs, axis=0, keepdims=True)
        grad_score = (probs * (grad_probs - row_dot) * scale).astype(BF16)
        probs_low = probs.astype(BF16)
        grad_value = jnp.dot(probs_low, grad_stack, preferred_element_type=F32)
        grad_key = jnp.dot(grad_score, query_stack, preferred_element_type=F32)
        key_t, value_t = key.T, value.T

        def per_head(left, right):
            parts = []
            for h in range(HEADS_PER_GROUP):
                rows = slice(h * HEAD_DIM, (h + 1) * HEAD_DIM)
                lanes = slice(h * GROUP_LANES, (h + 1) * GROUP_LANES)
                parts.append(jnp.dot(left[rows], right[:, lanes], preferred_element_type=F32))
            return jnp.concatenate(parts, axis=0).T[:count].astype(BF16)

        results[keys, columns(0)] = per_head(value_t, probs_low)
        results[keys, columns(1)] = per_head(key_t, grad_score)
        results[keys, columns(2)] = grad_key.astype(BF16)
        results[keys, columns(3)] = grad_value.astype(BF16)


def finish(rows, results, gain, w_query, w_key_value, w_out):
    width = rows.shape[1] // 2
    values, grads = rows[:, :width], rows[:, width:]
    block_output = values.astype(F32) + jnp.dot(results[:, :width], w_out[...], preferred_element_type=F32)
    grad_hidden = lax.dot_general(results[:, width : 2 * width], w_query[...], NT, preferred_element_type=F32)
    grad_hidden = grad_hidden + lax.dot_general(
        results[:, 2 * width :], w_key_value[...], NT, preferred_element_type=F32
    )
    unit, inv_dev = normalized(values)
    scaled = grad_hidden * gain[...]
    centred = scaled - jnp.mean(scaled, axis=-1, keepdims=True)
    norm_grad = inv_dev * (centred - unit * jnp.mean(scaled * unit, axis=-1, keepdims=True))
    input_grad = grads.astype(F32) + norm_grad
    return jnp.concatenate([block_output.astype(BF16), input_grad.astype(BF16)], axis=1)


def window_kernel(
    kind, meta, code_column, code_row, own_rows, own_heads, far_rows, gain, bias, w_query, w_key_value, w_out,
    far_result, own_result, heads, results, bias_of
):
    width = far_rows.shape[1] // 2
    cut = SLOTS[0]
    side = 1 - meta[0] if kind == "same" else meta[0]
    frames = [meta[1 + side * WT + index] for index in range(WT)]
    place_column = lax.broadcasted_iota(jnp.int32, (PADDED_ROWS, 1), 0)
    place_row = lax.broadcasted_iota(jnp.int32, (1, PADDED_ROWS), 1)
    by_key = cell_codes(code_column[side], place_column, frames)
    by_query = cell_codes(code_row[side], place_row, frames)
    for unit in range(2):
        block = slice(unit * GROUP_LANES, (unit + 1) * GROUP_LANES)
        bias_of[block, :] = jnp.where(by_key[block] == by_query[:, block], 0.0, MASKED)

    heads[:cut] = own_heads[:cut]
    heads[FIRST : FIRST + SLOTS[1]] = own_heads[cut:]
    heads[WINDOW_ROWS:] = jnp.zeros((PADDED_ROWS - WINDOW_ROWS, heads.shape[1]), BF16)

    def store(column, result):
        columns = slice(column, column + result.shape[1])
        heads[cut:FIRST, columns] = result[:cut]
        heads[FIRST + SLOTS[1] : WINDOW_ROWS, columns] = result[cut:]

    project(far_rows[:, :width], far_rows[:, width:], gain, bias, w_query, w_key_value, w_out, store)

    def body(group, carry):
        attend(heads, results, bias_of, group, width)
        return carry

    lax.fori_loop(0, width // GROUP_LANES, body, 0)

    far = jnp.concatenate([results[cut:FIRST], results[FIRST + SLOTS[1] : WINDOW_ROWS]], axis=0)
    own = jnp.concatenate([results[:cut], results[FIRST : FIRST + SLOTS[1]]], axis=0)
    if kind == "same":
        both = finish(
            jnp.concatenate([far_rows[...], own_rows[...]], axis=0),
            jnp.concatenate([far, own], axis=0),
            gain, w_query, w_key_value, w_out,
        )
        far_result[...] = both[:ROWS]
        own_result[...] = both[ROWS:]
    else:
        far_result[...] = finish(far_rows[...], far, gain, w_query, w_key_value, w_out)
        own_result[...] = own


def tail_kernel(rows, results, gain, w_query, w_key_value, w_out, out):
    out[...] = finish(rows[...], results[...], gain, w_query, w_key_value, w_out)


def unpack_kernel(meta, table, own_same, own_cross, far_same, far_cross, block_output, input_grad):
    width = block_output.shape[1]
    token = lax.broadcasted_iota(jnp.int32, (block_output.shape[0], 4 * ROWS), 0)
    one_hot = (token == table[meta[0]]).astype(F32).astype(BF16)
    values = jnp.concatenate([own_same[...], own_cross[...], far_same[...], far_cross[...]], axis=0)
    block_output[...] = picked(one_hot, values[:, :width])
    input_grad[...] = picked(one_hot, values[:, width:])


def call(kernel, out_shapes, *operands, scratch=(), flops=0, megabytes=24):
    smem = pl.BlockSpec(memory_space=pltpu.SMEM)
    vmem = pl.BlockSpec(memory_space=pltpu.VMEM)
    outs = [jax.ShapeDtypeStruct(shape, BF16) for shape in out_shapes]
    moved = sum(x.size * x.dtype.itemsize for x in operands) + sum(x.size * 2 for x in outs)
    return pl.pallas_call(
        kernel,
        out_shape=outs,
        in_specs=[smem if x.ndim == 1 and x.dtype == jnp.int32 else vmem for x in operands],
        out_specs=[vmem] * len(outs),
        scratch_shapes=list(scratch),
        compiler_params=pltpu.CompilerParams(vmem_limit_bytes=megabytes << 20),
        cost_estimate=pl.CostEstimate(flops=flops, bytes_accessed=moved, transcendentals=0),
    )(*operands)


def on_device(inputs, out_grad, live_rows, live_cols, norm_gain, norm_bias, w_query, w_key_value, w_out):
    token_count, width = inputs.shape
    count = lax.axis_size("seq")
    position = lax.axis_index("seq")
    parity = position % 2

    frame_total = count * WT
    words = live_rows * 256 + live_cols * 16 + (jnp.arange(frame_total, dtype=jnp.int32) < HALF).astype(jnp.int32)
    around = jnp.concatenate([words[-HALF:], words, words[:HALF]])
    meta = jnp.concatenate([parity.reshape(1), lax.dynamic_slice(around, (position * WT,), (2 * WT,))])

    gain, bias = norm_gain.reshape(1, width), norm_bias.reshape(1, width)
    weights = (w_query, w_key_value, w_out)
    own_table, send_table = jnp.asarray(OWN_TOKENS[..., None]), jnp.asarray(SEND_TOKENS[..., None])
    unpack_table = jnp.asarray(np.concatenate([OWN_TOKENS, SEND_TOKENS], axis=1)[:, None, :])
    code_column, code_row = jnp.asarray(WINDOW_CODES[..., None]), jnp.asarray(WINDOW_CODES[:, None, :])

    pair = [(i, i ^ 1) for i in range(count)]
    across = [(i, (i + 1) % count if i % 2 else (i - 1) % count) for i in range(count)]

    rows_shape, heads_shape = (ROWS, 2 * width), (ROWS, 4 * width)
    product = 2 * width * width
    send_same, send_cross = call(
        pack_kernel, [rows_shape] * 2, meta, send_table, inputs, out_grad, flops=4 * ROWS * token_count * 2 * width
    )
    far_cross_rows = lax.ppermute(send_cross, "seq", across)
    far_same_rows = lax.ppermute(send_same, "seq", pair)
    own_same_rows, own_cross_rows, own_same_heads, own_cross_heads = call(
        own_kernel, [rows_shape] * 2 + [heads_shape] * 2, meta, own_table, inputs, out_grad, gain, bias, *weights,
        flops=2 * ROWS * 5 * product,
    )
    scratch = (
        pltpu.VMEM((PADDED_ROWS, 4 * width), BF16),
        pltpu.VMEM((PADDED_ROWS, 4 * width), BF16),
        pltpu.VMEM((PADDED_ROWS, GROUP_LANES), F32),
    )

    def window(kind, own_rows, own_heads, far_rows):
        return call(
            functools.partial(window_kernel, kind), [rows_shape, rows_shape if kind == "same" else heads_shape],
            meta, code_column, code_row, own_rows, own_heads, far_rows, gain, bias, *weights,
            scratch=scratch, flops=2 * ROWS * 10 * product,
        )

    far_same, own_same = window("same", own_same_rows, own_same_heads, far_same_rows)
    back_same = lax.ppermute(far_same, "seq", pair)
    far_cross, own_cross_heads = window("cross", own_cross_rows, own_cross_heads, far_cross_rows)
    back_cross = lax.ppermute(far_cross, "seq", across)
    own_cross, = call(
        tail_kernel, [rows_shape], own_cross_rows, own_cross_heads, gain, *weights, flops=ROWS * 4 * product
    )
    return tuple(
        call(
            unpack_kernel, [(token_count, width)] * 2, meta, unpack_table, own_same, own_cross, back_same, back_cross,
            flops=8 * ROWS * token_count * 2 * width,
        )
    )


def solution(mesh):
    rows = P(("group", "seq"), None)
    in_specs = (rows, rows, P("group"), P("group"), P(), P(), P(), P(), P())
    return jax.shard_map(on_device, mesh=mesh, in_specs=in_specs, out_specs=(rows, rows), check_vma=False)
```

```python
import functools

import jax
import jax.numpy as jnp
import numpy as np
from jax import lax
from jax.experimental import pallas as pl
from jax.experimental.pallas import tpu as pltpu
from jax.sharding import PartitionSpec as P

HEAD_DIM = 32
WT = 8
WH = 7
WW = 7
CELLS = WH * WW
HALF = WT // 2
EPSILON = 1e-05
GROUP_LANES = 128
HEADS_PER_GROUP = GROUP_LANES // HEAD_DIM
SLOTS = (64, 48)
ROWS = sum(SLOTS)
FIRST = 2 * SLOTS[0]
SECOND = 2 * SLOTS[1]
WINDOW_ROWS = FIRST + SECOND
PADDED_ROWS = 2 * GROUP_LANES
MASKED = -1e30
SCALE = HEAD_DIM ** (-0.5)
LOG2E = float(np.log2(np.e))
BF16 = jnp.bfloat16
F32 = jnp.float32
NT = (((1,), (1,)), ((), ()))


def quadrant_cells(quadrant):
    rows = range(WH // 2) if quadrant & 2 else range(WH // 2, WH)
    cols = range(WW // 2) if quadrant & 1 else range(WW // 2, WW)
    return [(row, col) for row in rows for col in cols]


def half_slots(units):
    slots = []
    for quadrant, room in zip(units, SLOTS):
        entries = [(frame, row, col) for frame in range(HALF) for row, col in quadrant_cells(quadrant)]
        slots += entries + [None] * (room - len(entries))
    return slots


def tables():
    takes = {"last": (0, 3), "first": (1, 2)}
    gives = {"last": (1, 2), "first": (0, 3)}

    def tokens(side, units):
        shift = HALF if side == "last" else 0
        return [-1 if s is None else (s[0] + shift) * CELLS + s[1] * WW + s[2] for s in half_slots(units)]

    def codes(slots, second_half):
        return [-1 if s is None else (s[0] + HALF * second_half) * 64 + s[1] * 8 + s[2] for s in slots]

    own, send, window = [], [], []
    for parity in range(2):
        sides = ("last", "first") if parity == 0 else ("first", "last")
        own.append(sum((tokens(side, takes[side]) for side in sides), []))
        send.append(sum((tokens(side, gives[side]) for side in sides), []))
    for side in ("first", "last"):
        slots = half_slots(takes[side])
        mine = codes(slots, side == "first")
        theirs = codes(slots, side == "last")
        cut = SLOTS[0]
        rows = mine[:cut] + theirs[:cut] + mine[cut:] + theirs[cut:]
        window.append(rows + [-1] * (PADDED_ROWS - len(rows)))
    return np.array(own, np.int32), np.array(send, np.int32), np.array(window, np.int32)


OWN_TOKENS, SEND_TOKENS, WINDOW_CODES = tables()


def normalized(values_in):
    values = values_in.astype(F32)
    centred = values - jnp.mean(values, axis=-1, keepdims=True)
    inv_dev = lax.rsqrt(jnp.mean(centred * centred, axis=-1, keepdims=True) + EPSILON)
    return centred * inv_dev, inv_dev


def one_hot_rows(token_column, token_count):
    lanes = lax.broadcasted_iota(jnp.int32, (token_column.shape[0], token_count), 1)
    return (lanes == token_column).astype(F32).astype(BF16)


def picked(one_hot, values):
    return jnp.dot(one_hot, values, preferred_element_type=F32).astype(BF16)


def side_of(kind, position):
    parity = lax.rem(position, 2)
    return 1 - parity if kind == "same" else parity


def pack_kernel(position, table, inputs, out_grad, same, cross, values, grads, sems):
    width = inputs.shape[1]
    copies = [
        pltpu.make_async_copy(source, target, sems.at[place])
        for place, (source, target) in enumerate(((inputs, values), (out_grad, grads)))
    ]
    for copy in copies:
        copy.start()
    one_hot = one_hot_rows(table[lax.rem(position[0], 2)], inputs.shape[0])
    for place, source in enumerate((values, grads)):
        copies[place].wait()
        rows = picked(one_hot, source[...])
        columns = slice(place * width, (place + 1) * width)
        same[:, columns] = rows[:ROWS]
        cross[:, columns] = rows[ROWS:]


def hidden_of(values, gain, bias):
    unit, _ = normalized(values)
    return (unit * gain[...] + bias[...]).astype(BF16)


def own_kernel(
    position, table, inputs, out_grad, gain, bias, w_query, w_key_value, w_out,
    rows_same, rows_cross, heads_same, heads_cross, query_copy, pair_copy, out_copy, sems,
):
    width = inputs.shape[1]
    halves = [pl.ds(part * width, width) for part in range(2)]
    copies = [pltpu.make_async_copy(w_query, query_copy, sems.at[0])]
    copies += [
        pltpu.make_async_copy(w_key_value.at[:, part], pair_copy.at[:, part], sems.at[1 + index])
        for index, part in enumerate(halves)
    ]
    copies += [pltpu.make_async_copy(w_out, out_copy, sems.at[3])]
    for copy in copies:
        copy.start()
    one_hot = one_hot_rows(table[lax.rem(position[0], 2)], inputs.shape[0])
    values = picked(one_hot, inputs[...])
    hidden = hidden_of(values, gain, bias)
    grads = picked(one_hot, out_grad[...])
    for place, rows in enumerate((values, grads)):
        columns = slice(place * width, (place + 1) * width)
        rows_same[:, columns] = rows[:ROWS]
        rows_cross[:, columns] = rows[ROWS:]
    for part in range(3):
        copies[part].wait()
        weights = query_copy[...] if part == 0 else pair_copy[:, halves[part - 1]]
        result = jnp.dot(hidden, weights, preferred_element_type=F32).astype(BF16)
        columns = slice(part * width, (part + 1) * width)
        heads_same[:, columns] = result[:ROWS]
        heads_cross[:, columns] = result[ROWS:]
    copies[3].wait()


def cell_codes(slots, place, frames):
    frame = slots >> 6
    word = jnp.zeros_like(slots)
    for index, frame_word in enumerate(frames):
        word = jnp.where(frame == index, frame_word, word)
    row, col = (slots >> 3) & 7, slots & 7
    live = (slots >= 0) & (row < (word >> 8)) & (col < ((word >> 4) & 15))
    return jnp.where(live, word & 1, -1 - place)


def head_rows(h):
    return slice(h * HEAD_DIM, (h + 1) * HEAD_DIM)


def head_lanes(h):
    return slice(h * GROUP_LANES, (h + 1) * GROUP_LANES)


def block_diagonal(values):
    zero = jnp.zeros((HEAD_DIM, GROUP_LANES), values.dtype)
    return jnp.concatenate(
        [
            jnp.concatenate([values[head_rows(r)] if r == h else zero for r in range(HEADS_PER_GROUP)], axis=0)
            for h in range(HEADS_PER_GROUP)
        ],
        axis=1,
    )


def score_stage(unit, group, groups, count, heads, grads_t, query_t, scores, grad_probs):
    base = unit * GROUP_LANES
    keys = slice(base, base + count)
    query = heads[group, base : base + GROUP_LANES].T
    query_t[...] = query
    grad = grads_t[unit, pl.ds(pl.multiple_of(group * GROUP_LANES, GROUP_LANES), GROUP_LANES)]
    score = jnp.dot(heads[groups + group, keys], block_diagonal(query), preferred_element_type=F32)
    grad_prob = jnp.dot(heads[2 * groups + group, keys], block_diagonal(grad), preferred_element_type=F32)
    for h in range(HEADS_PER_GROUP):
        scores[h] = score[:, head_lanes(h)]
        grad_probs[h] = grad_prob[:, head_lanes(h)]


def softmax_stage(unit, count, bias_of, scores, grad_probs, probs, grad_scores):
    for h in range(HEADS_PER_GROUP):
        score = scores[h] * (SCALE * LOG2E) + bias_of[unit, :count]
        raw = jnp.exp2(score - jnp.max(score, axis=0, keepdims=True))
        inverse = 1.0 / jnp.sum(raw, axis=0, keepdims=True)
        grad_prob = grad_probs[h]
        row_dot = jnp.sum(raw * grad_prob, axis=0, keepdims=True) * inverse
        probs[h] = (raw * inverse).astype(BF16)
        grad_scores[h] = (raw * ((grad_prob - row_dot) * (inverse * SCALE))).astype(BF16)


def product_stage(unit, group, groups, count, heads, grads_t, query_t, probs, grad_scores, results):
    base = unit * GROUP_LANES
    keys = slice(base, base + count)
    grad = grads_t[unit, pl.ds(pl.multiple_of(group * GROUP_LANES, GROUP_LANES), GROUP_LANES)]
    key_t, value_t = heads[groups + group, keys].T, heads[2 * groups + group, keys].T

    def per_key(left, right):
        left = jnp.concatenate([left[h] for h in range(HEADS_PER_GROUP)], axis=1)
        return lax.dot_general(left, block_diagonal(right), NT, preferred_element_type=F32).astype(BF16)

    def per_query(left, right):
        parts = [jnp.dot(left[head_rows(h)], right[h], preferred_element_type=F32) for h in range(HEADS_PER_GROUP)]
        return jnp.concatenate(parts, axis=0).T[:count].astype(BF16)

    results[group, keys] = per_query(value_t, probs)
    results[groups + group, keys] = per_query(key_t, grad_scores)
    results[2 * groups + group, keys] = per_key(grad_scores, query_t[...])
    results[3 * groups + group, keys] = per_key(probs, grad)


def finish(values, grads, results, gain, w_query, w_key_value, w_out):
    width = values.shape[1]
    rows = values.shape[0]
    block_output = values.astype(F32) + jnp.dot(results[:, :width], w_out[...], preferred_element_type=F32)
    fill = -rows % GROUP_LANES
    moves = jnp.concatenate([results[:, width:], jnp.zeros((fill, 3 * width), BF16)], axis=0)
    grad_hidden = lax.dot_general(w_query[...], moves[:, :width], NT, preferred_element_type=F32)
    grad_hidden = grad_hidden + lax.dot_general(w_key_value[...], moves[:, width:], NT, preferred_element_type=F32)
    grad_hidden = grad_hidden.T[:rows]
    unit, inv_dev = normalized(values)
    scaled = grad_hidden * gain[...]
    centred = scaled - jnp.mean(scaled, axis=-1, keepdims=True)
    norm_grad = inv_dev * (centred - unit * jnp.mean(scaled * unit, axis=-1, keepdims=True))
    return block_output.astype(BF16), (grads.astype(F32) + norm_grad).astype(BF16)


def window_kernel(
    kind, position, live_rows, live_cols, code_column, code_row, own_rows, own_heads, far_rows, other_far,
    gain, bias, w_query, w_key_value, w_out, far_result, own_moves, other_heads,
    heads, window_grads, grads_t, results, bias_of, query_t0, query_t1, *stages,
):
    width = far_rows.shape[1] // 2
    groups = width // GROUP_LANES
    cut, second = SLOTS[0], FIRST + SLOTS[1]
    side = side_of(kind, position[0])
    total = live_rows.shape[0]
    frames = []
    for index in range(WT):
        frame = lax.rem(position[0] * WT + (side * 2 - 1) * HALF + index + total, total)
        frames.append(live_rows[frame] * 256 + live_cols[frame] * 16 + (frame < HALF).astype(jnp.int32))
    by_key = cell_codes(code_column[side], lax.broadcasted_iota(jnp.int32, (PADDED_ROWS, 1), 0), frames)
    by_query = cell_codes(code_row[side], lax.broadcasted_iota(jnp.int32, (1, PADDED_ROWS), 1), frames)
    for unit in range(2):
        block = slice(unit * GROUP_LANES, (unit + 1) * GROUP_LANES)
        bias_of[unit] = jnp.where(by_key[block] == by_query[:, block], 0.0, MASKED)

    window_grads[:cut] = own_rows[:cut, width:]
    window_grads[cut:FIRST] = far_rows[:cut, width:]
    window_grads[FIRST:second] = own_rows[cut:, width:]
    window_grads[second:WINDOW_ROWS] = far_rows[cut:, width:]
    window_grads[WINDOW_ROWS:] = jnp.zeros((PADDED_ROWS - WINDOW_ROWS, width), BF16)
    turned = lax.dot_general(w_out[...], window_grads[...], NT, preferred_element_type=F32).astype(BF16)
    for unit in range(2):
        grads_t[unit] = turned[:, unit * GROUP_LANES : (unit + 1) * GROUP_LANES]

    def place(block, own, far):
        heads[block, :cut] = own[:cut]
        heads[block, cut:FIRST] = far[:cut]
        heads[block, FIRST:second] = own[cut:]
        heads[block, second:WINDOW_ROWS] = far[cut:]

    for block in range(groups):
        heads[block, WINDOW_ROWS:] = jnp.zeros((PADDED_ROWS - WINDOW_ROWS, GROUP_LANES), BF16)
    if kind == "cross":
        hidden = hidden_of(jnp.concatenate([far_rows[:, :width], other_far[:, :width]], axis=0), gain, bias)
    for part in range(3):
        columns = slice(part * width, (part + 1) * width)
        if kind == "cross":
            weights = w_query[...] if part == 0 else w_key_value[:, slice((part - 1) * width, part * width)]
            result = jnp.dot(hidden, weights, preferred_element_type=F32).astype(BF16)
            far = result[:ROWS]
            other_heads[:, columns] = result[ROWS:]
        else:
            far = other_far[:, columns]
        for group in range(groups):
            lanes = slice(group * GROUP_LANES, (group + 1) * GROUP_LANES)
            first = part * width + group * GROUP_LANES
            place(part * groups + group, own_heads[:, first : first + GROUP_LANES], far[:, lanes])

    query_t = (query_t0, query_t1)
    counts = (FIRST, SECOND)
    scores, grad_probs, probs, grad_scores = stages[0:2], stages[2:4], stages[4:6], stages[6:8]

    def score(unit, group):
        score_stage(unit, group, groups, counts[unit], heads, grads_t, query_t[unit], scores[unit], grad_probs[unit])

    def softmax(unit):
        softmax_stage(unit, counts[unit], bias_of, scores[unit], grad_probs[unit], probs[unit], grad_scores[unit])

    def product(unit, group):
        product_stage(
            unit, group, groups, counts[unit], heads, grads_t, query_t[unit], probs[unit], grad_scores[unit], results
        )

    probs[1][...] = jnp.zeros_like(probs[1])
    grad_scores[1][...] = jnp.zeros_like(grad_scores[1])
    query_t[1][...] = jnp.zeros_like(query_t[1])
    score(0, 0)

    def body(group, carry):
        product(1, jnp.maximum(group - 1, 0))
        score(1, group)
        softmax(0)
        product(0, group)
        score(0, jnp.minimum(group + 1, groups - 1))
        softmax(1)
        return carry

    lax.fori_loop(0, groups, body, 0)
    product(1, groups - 1)

    def rows_of(first, last):
        return jnp.concatenate(
            [
                jnp.concatenate([results[block, first[0] : first[1]], results[block, last[0] : last[1]]], axis=0)
                for block in range(4 * groups)
            ],
            axis=1,
        )

    own_moves[...] = rows_of((0, cut), (FIRST, second))
    block_output, input_grad = finish(
        far_rows[:, :width], far_rows[:, width:], rows_of((cut, FIRST), (second, WINDOW_ROWS)),
        gain, w_query, w_key_value, w_out,
    )
    far_result[:, :width] = block_output
    far_result[:, width:] = input_grad


def tail_kernel(rows_same, rows_cross, moves_same, moves_cross, gain, w_query, w_key_value, w_out, out):
    width = rows_same.shape[1] // 2
    rows = jnp.concatenate([rows_same[...], rows_cross[...]], axis=0)
    moves = jnp.concatenate([moves_same[...], moves_cross[...]], axis=0)
    block_output, input_grad = finish(rows[:, :width], rows[:, width:], moves, gain, w_query, w_key_value, w_out)
    out[:, :width] = block_output
    out[:, width:] = input_grad


def unpack_kernel(position, table, own, far_same, far_cross, block_output, input_grad, outputs, sems):
    width = block_output.shape[1]
    chunk = width // 2
    token = lax.broadcasted_iota(jnp.int32, (block_output.shape[0], 4 * ROWS), 0)
    one_hot = (token == table[lax.rem(position[0], 2)]).astype(F32).astype(BF16)
    copies = []
    for index in range(4):
        columns = slice(index * chunk, (index + 1) * chunk)
        values = jnp.concatenate([own[:, columns], far_same[:, columns], far_cross[:, columns]], axis=0)
        outputs[index] = picked(one_hot, values)
        target = block_output if index < 2 else input_grad
        copies.append(
            pltpu.make_async_copy(outputs.at[index], target.at[:, pl.ds(index % 2 * chunk, chunk)], sems.at[index])
        )
        copies[-1].start()
    for copy in copies:
        copy.wait()


SMEM, VMEM, HBM = pltpu.SMEM, pltpu.VMEM, pltpu.HBM


def call(kernel, outs, *operands, scratch=(), flops=0, megabytes=24):
    spaces, operands = zip(*operands)
    out_spaces, shapes = zip(*outs)
    outs = [jax.ShapeDtypeStruct(shape, BF16) for shape in shapes]
    moved = sum(x.size * x.dtype.itemsize for x in operands) + sum(x.size * 2 for x in outs)
    return pl.pallas_call(
        kernel,
        out_shape=outs,
        in_specs=[pl.BlockSpec(memory_space=space) for space in spaces],
        out_specs=[pl.BlockSpec(memory_space=space) for space in out_spaces],
        scratch_shapes=list(scratch),
        compiler_params=pltpu.CompilerParams(vmem_limit_bytes=megabytes << 20),
        cost_estimate=pl.CostEstimate(flops=flops, bytes_accessed=moved, transcendentals=0),
    )(*operands)


def on_device(inputs, out_grad, live_rows, live_cols, norm_gain, norm_bias, w_query, w_key_value, w_out):
    token_count, width = inputs.shape
    groups = width // GROUP_LANES
    count = lax.axis_size("seq")
    position = (SMEM, lax.axis_index("seq").reshape(1))
    live = ((SMEM, live_rows), (SMEM, live_cols))
    norm = ((VMEM, norm_gain.reshape(1, width)), (VMEM, norm_bias.reshape(1, width)))
    own_table, send_table = (VMEM, jnp.asarray(OWN_TOKENS[..., None])), (VMEM, jnp.asarray(SEND_TOKENS[..., None]))
    unpack_table = (VMEM, jnp.asarray(np.concatenate([OWN_TOKENS, SEND_TOKENS], axis=1)[:, None, :]))
    codes = (VMEM, jnp.asarray(WINDOW_CODES[..., None])), (VMEM, jnp.asarray(WINDOW_CODES[:, None, :]))

    pair = [(i, i ^ 1) for i in range(count)]
    across = [(i, (i + 1) % count if i % 2 else (i - 1) % count) for i in range(count)]

    rows_out, heads_out, moves_out = (VMEM, (ROWS, 2 * width)), (VMEM, (ROWS, 3 * width)), (VMEM, (ROWS, 4 * width))
    product = 2 * width * width
    send_same, send_cross, values, grads = call(
        pack_kernel,
        [rows_out] * 2 + [(VMEM, inputs.shape)] * 2,
        position, send_table, (HBM, inputs), (HBM, out_grad),
        scratch=[pltpu.SemaphoreType.DMA((2,))],
        flops=4 * ROWS * token_count * 2 * width,
    )
    far_cross_rows = lax.ppermute(send_cross, "seq", across)
    far_same_rows = lax.ppermute(send_same, "seq", pair)
    own_same_rows, own_cross_rows, own_same_heads, own_cross_heads, *weights = call(
        own_kernel,
        [rows_out] * 2 + [heads_out] * 2 + [(VMEM, w.shape) for w in (w_query, w_key_value, w_out)],
        position, own_table, (VMEM, values), (VMEM, grads), *norm, (HBM, w_query), (HBM, w_key_value), (HBM, w_out),
        scratch=[pltpu.SemaphoreType.DMA((4,))],
        flops=2 * ROWS * 4 * product,
    )
    weights = [(VMEM, w) for w in weights]

    stages = [VMEM((HEADS_PER_GROUP, n, GROUP_LANES), kind) for kind in (F32, F32, BF16, BF16) for n in (FIRST, SECOND)]
    scratch = [
        VMEM((3 * groups, PADDED_ROWS, GROUP_LANES), BF16),
        VMEM((PADDED_ROWS, width), BF16),
        VMEM((2, width, GROUP_LANES), BF16),
        VMEM((4 * groups, PADDED_ROWS, GROUP_LANES), BF16),
        VMEM((2, GROUP_LANES, GROUP_LANES), F32),
        VMEM((GROUP_LANES, GROUP_LANES), BF16),
        VMEM((GROUP_LANES, GROUP_LANES), BF16),
        *stages,
    ]

    def window(kind, own_rows, own_heads, far_rows, other_far):
        outs = [rows_out, moves_out, heads_out if kind == "cross" else (VMEM, (16, GROUP_LANES))]
        arrays = [(VMEM, x) for x in (own_rows, own_heads, far_rows, other_far)]
        return call(
            functools.partial(window_kernel, kind), outs, position, *live, *codes, *arrays, *norm, *weights,
            scratch=scratch, flops=2 * ROWS * 10 * product,
        )

    far_cross, own_cross_moves, far_same_heads = window(
        "cross", own_cross_rows, own_cross_heads, far_cross_rows, far_same_rows
    )
    back_cross = lax.ppermute(far_cross, "seq", across)
    far_same, own_same_moves, _ = window("same", own_same_rows, own_same_heads, far_same_rows, far_same_heads)
    back_same = lax.ppermute(far_same, "seq", pair)
    arrays = [(VMEM, x) for x in (own_same_rows, own_cross_rows, own_same_moves, own_cross_moves)]
    (own,) = call(
        tail_kernel, [(VMEM, (2 * ROWS, 2 * width))], *arrays, norm[0], *weights, flops=2 * ROWS * 4 * product
    )
    arrays = [(VMEM, x) for x in (own, back_same, back_cross)]
    return tuple(
        call(
            unpack_kernel, [(HBM, (token_count, width))] * 2, position, unpack_table, *arrays,
            scratch=[VMEM((4, token_count, width // 2), BF16), pltpu.SemaphoreType.DMA((4,))],
            flops=8 * ROWS * token_count * 2 * width,
        )
    )


def solution(mesh):
    rows = P(("group", "seq"), None)
    in_specs = (rows, rows, P("group"), P("group"), P(), P(), P(), P(), P())
    return jax.shard_map(on_device, mesh=mesh, in_specs=in_specs, out_specs=(rows, rows), check_vma=False)
```

```python
import functools

import jax
import jax.numpy as jnp
import numpy as np
from jax import lax
from jax.experimental import pallas as pl
from jax.experimental.pallas import tpu as pltpu
from jax.sharding import PartitionSpec as P


HEAD_DIM = 32
WT = 8
WH = 7
WW = 7
CELLS = WH * WW
HALF = WT // 2
EPSILON = 1e-05
GROUP_LANES = 128
HEADS_PER_GROUP = GROUP_LANES // HEAD_DIM
SLOTS = (64, 48)
ROWS = sum(SLOTS)
FIRST = 2 * SLOTS[0]
SECOND = 2 * SLOTS[1]
WINDOW_ROWS = FIRST + SECOND
PADDED_ROWS = 2 * GROUP_LANES
MASKED = -1e30
SCALE = HEAD_DIM ** (-0.5)
LOG2E = float(np.log2(np.e))
BF16 = jnp.bfloat16
F32 = jnp.float32
NT = (((1,), (1,)), ((), ()))


def quadrant_cells(quadrant):
    rows = range(WH // 2) if quadrant & 2 else range(WH // 2, WH)
    cols = range(WW // 2) if quadrant & 1 else range(WW // 2, WW)
    return [(row, col) for row in rows for col in cols]


def half_slots(units):
    slots = []
    for quadrant, room in zip(units, SLOTS):
        entries = [(frame, row, col) for frame in range(HALF) for row, col in quadrant_cells(quadrant)]
        slots += entries + [None] * (room - len(entries))
    return slots


def tables():
    takes = {"last": (0, 3), "first": (1, 2)}
    gives = {"last": (1, 2), "first": (0, 3)}

    def tokens(side, units):
        shift = HALF if side == "last" else 0
        return [-1 if s is None else (s[0] + shift) * CELLS + s[1] * WW + s[2] for s in half_slots(units)]

    def codes(slots, second_half):
        return [-1 if s is None else (s[0] + HALF * second_half) * 64 + s[1] * 8 + s[2] for s in slots]

    own, send, window = [], [], []
    for parity in range(2):
        sides = ("last", "first") if parity == 0 else ("first", "last")
        own.append(sum((tokens(side, takes[side]) for side in sides), []))
        send.append(sum((tokens(side, gives[side]) for side in sides), []))
    for side in ("first", "last"):
        slots = half_slots(takes[side])
        mine = codes(slots, side == "first")
        theirs = codes(slots, side == "last")
        cut = SLOTS[0]
        rows = mine[:cut] + theirs[:cut] + mine[cut:] + theirs[cut:]
        window.append(rows + [-1] * (PADDED_ROWS - len(rows)))
    return np.array(own, np.int32), np.array(send, np.int32), np.array(window, np.int32)


OWN_TOKENS, SEND_TOKENS, WINDOW_CODES = tables()


def normalized(values_in):
    values = values_in.astype(F32)
    centred = values - jnp.mean(values, axis=-1, keepdims=True)
    inv_dev = lax.rsqrt(jnp.mean(centred * centred, axis=-1, keepdims=True) + EPSILON)
    return centred * inv_dev, inv_dev


def one_hot_rows(token_column, token_count):
    lanes = lax.broadcasted_iota(jnp.int32, (token_column.shape[0], token_count), 1)
    return (lanes == token_column).astype(F32).astype(BF16)


def picked(one_hot, values):
    return jnp.dot(one_hot, values, preferred_element_type=F32).astype(BF16)


def side_of(kind, position):
    parity = lax.rem(position, 2)
    return 1 - parity if kind == "same" else parity


def pack_kernel(
    position, send_table, own_table, inputs, out_grad, same, cross, values, grads, own_rows, send_rows, sems
):
    width = inputs.shape[1]
    moves = ((send_table, send_rows), (inputs, values), (out_grad, grads), (own_table, own_rows))
    copies = [pltpu.make_async_copy(source, target, sems.at[place]) for place, (source, target) in enumerate(moves)]
    for copy in copies:
        copy.start()
    copies[0].wait()
    one_hot = one_hot_rows(send_rows[lax.rem(position[0], 2)], inputs.shape[0])
    for place, source in enumerate((values, grads)):
        copies[1 + place].wait()
        rows = picked(one_hot, source[...])
        columns = slice(place * width, (place + 1) * width)
        same[:, columns] = rows[:ROWS]
        cross[:, columns] = rows[ROWS:]
    copies[3].wait()


def hidden_of(values, gain, bias):
    unit, _ = normalized(values)
    return (unit * gain[...] + bias[...]).astype(BF16)


def own_kernel(
    position, table, inputs, out_grad, w_query, w_key_value, w_out, gain, bias, code_column, code_row, unpack_table,
    rows_same, rows_cross, heads_same, heads_cross, query_copy, pair_copy, out_copy, gain_copy, bias_copy,
    column_copy, row_copy, unpack_copy, sems,
):
    width = inputs.shape[1]
    halves = [pl.ds(part * width, width) for part in range(2)]
    moves = [(gain, gain_copy), (bias, bias_copy), (w_query, query_copy)]
    moves += [(w_key_value.at[:, part], pair_copy.at[:, part]) for part in halves]
    moves += [(w_out, out_copy), (code_column, column_copy), (code_row, row_copy), (unpack_table, unpack_copy)]
    copies = [pltpu.make_async_copy(source, target, sems.at[place]) for place, (source, target) in enumerate(moves)]
    for copy in copies:
        copy.start()
    one_hot = one_hot_rows(table[lax.rem(position[0], 2)], inputs.shape[0])
    values = picked(one_hot, inputs[...])
    copies[0].wait()
    copies[1].wait()
    hidden = hidden_of(values, gain_copy, bias_copy)
    grads = picked(one_hot, out_grad[...])
    for place, rows in enumerate((values, grads)):
        columns = slice(place * width, (place + 1) * width)
        rows_same[:, columns] = rows[:ROWS]
        rows_cross[:, columns] = rows[ROWS:]
    for part in range(3):
        copies[2 + part].wait()
        weights = query_copy[...] if part == 0 else pair_copy[:, halves[part - 1]]
        result = jnp.dot(hidden, weights, preferred_element_type=F32).astype(BF16)
        columns = slice(part * width, (part + 1) * width)
        heads_same[:, columns] = result[:ROWS]
        heads_cross[:, columns] = result[ROWS:]
    for copy in copies[5:]:
        copy.wait()


def cell_codes(slots, place, frames):
    frame = slots >> 6
    word = jnp.zeros_like(slots)
    for index, frame_word in enumerate(frames):
        word = jnp.where(frame == index, frame_word, word)
    row, col = (slots >> 3) & 7, slots & 7
    live = (slots >= 0) & (row < (word >> 8)) & (col < ((word >> 4) & 15))
    return jnp.where(live, word & 1, -1 - place)


def head_rows(h):
    return slice(h * HEAD_DIM, (h + 1) * HEAD_DIM)


def head_lanes(h):
    return slice(h * GROUP_LANES, (h + 1) * GROUP_LANES)


def block_diagonal(values):
    zero = jnp.zeros((HEAD_DIM, GROUP_LANES), values.dtype)
    return jnp.concatenate(
        [
            jnp.concatenate([values[head_rows(r)] if r == h else zero for r in range(HEADS_PER_GROUP)], axis=0)
            for h in range(HEADS_PER_GROUP)
        ],
        axis=1,
    )


def score_stage(unit, group, groups, count, heads, grads_t, query_t, scores, grad_probs):
    base = unit * GROUP_LANES
    keys = slice(base, base + count)
    query = heads[group, base : base + GROUP_LANES].T
    query_t[...] = query
    grad = grads_t[unit, pl.ds(pl.multiple_of(group * GROUP_LANES, GROUP_LANES), GROUP_LANES)]
    score = jnp.dot(heads[groups + group, keys], block_diagonal(query), preferred_element_type=F32)
    grad_prob = jnp.dot(heads[2 * groups + group, keys], block_diagonal(grad), preferred_element_type=F32)
    for h in range(HEADS_PER_GROUP):
        scores[h] = score[:, head_lanes(h)]
        grad_probs[h] = grad_prob[:, head_lanes(h)]


def softmax_stage(unit, count, bias_of, scores, grad_probs, probs, grad_scores):
    for h in range(HEADS_PER_GROUP):
        score = scores[h] * (SCALE * LOG2E) + bias_of[unit, :count]
        raw = jnp.exp2(score - jnp.max(score, axis=0, keepdims=True))
        inverse = 1.0 / jnp.sum(raw, axis=0, keepdims=True)
        grad_prob = grad_probs[h]
        row_dot = jnp.sum(raw * grad_prob, axis=0, keepdims=True) * inverse
        probs[h] = (raw * inverse).astype(BF16)
        grad_scores[h] = (raw * ((grad_prob - row_dot) * (inverse * SCALE))).astype(BF16)


def product_stage(unit, group, groups, count, heads, grads_t, query_t, probs, grad_scores, results):
    base = unit * GROUP_LANES
    keys = slice(base, base + count)
    grad = grads_t[unit, pl.ds(pl.multiple_of(group * GROUP_LANES, GROUP_LANES), GROUP_LANES)]
    key_t, value_t = heads[groups + group, keys].T, heads[2 * groups + group, keys].T

    def per_key(left, right):
        left = jnp.concatenate([left[h] for h in range(HEADS_PER_GROUP)], axis=1)
        return lax.dot_general(left, block_diagonal(right), NT, preferred_element_type=F32).astype(BF16)

    def per_query(left, right):
        parts = [jnp.dot(left[head_rows(h)], right[h], preferred_element_type=F32) for h in range(HEADS_PER_GROUP)]
        return jnp.concatenate(parts, axis=0).T[:count].astype(BF16)

    results[group, keys] = per_query(value_t, probs)
    results[groups + group, keys] = per_query(key_t, grad_scores)
    results[2 * groups + group, keys] = per_key(grad_scores, query_t[...])
    results[3 * groups + group, keys] = per_key(probs, grad)


def finish(values, grads, results, gain, w_query, w_key_value, w_out):
    width = values.shape[1]
    rows = values.shape[0]
    block_output = values.astype(F32) + jnp.dot(results[:, :width], w_out[...], preferred_element_type=F32)
    fill = -rows % GROUP_LANES
    moves = jnp.concatenate([results[:, width:], jnp.zeros((fill, 3 * width), BF16)], axis=0)
    grad_hidden = lax.dot_general(w_query[...], moves[:, :width], NT, preferred_element_type=F32)
    grad_hidden = grad_hidden + lax.dot_general(w_key_value[...], moves[:, width:], NT, preferred_element_type=F32)
    grad_hidden = grad_hidden.T[:rows]
    unit, inv_dev = normalized(values)
    scaled = grad_hidden * gain[...]
    centred = scaled - jnp.mean(scaled, axis=-1, keepdims=True)
    norm_grad = inv_dev * (centred - unit * jnp.mean(scaled * unit, axis=-1, keepdims=True))
    return block_output.astype(BF16), (grads.astype(F32) + norm_grad).astype(BF16)


def window_kernel(
    kind, position, live_rows, live_cols, code_column, code_row, own_rows, own_heads, far_rows,
    gain, bias, w_query, w_key_value, w_out, far_result, own_moves,
    heads, window_grads, grads_t, results, bias_of, query_t0, query_t1, *stages,
):
    width = far_rows.shape[1] // 2
    groups = width // GROUP_LANES
    cut, second = SLOTS[0], FIRST + SLOTS[1]
    side = side_of(kind, position[0])
    total = live_rows.shape[0]
    frames = []
    for index in range(WT):
        frame = lax.rem(position[0] * WT + (side * 2 - 1) * HALF + index + total, total)
        frames.append(live_rows[frame] * 256 + live_cols[frame] * 16 + (frame < HALF).astype(jnp.int32))
    by_key = cell_codes(code_column[side], lax.broadcasted_iota(jnp.int32, (PADDED_ROWS, 1), 0), frames)
    by_query = cell_codes(code_row[side], lax.broadcasted_iota(jnp.int32, (1, PADDED_ROWS), 1), frames)
    for unit in range(2):
        block = slice(unit * GROUP_LANES, (unit + 1) * GROUP_LANES)
        bias_of[unit] = jnp.where(by_key[block] == by_query[:, block], 0.0, MASKED)

    window_grads[:cut] = own_rows[:cut, width:]
    window_grads[cut:FIRST] = far_rows[:cut, width:]
    window_grads[FIRST:second] = own_rows[cut:, width:]
    window_grads[second:WINDOW_ROWS] = far_rows[cut:, width:]
    window_grads[WINDOW_ROWS:] = jnp.zeros((PADDED_ROWS - WINDOW_ROWS, width), BF16)
    turned = lax.dot_general(w_out[...], window_grads[...], NT, preferred_element_type=F32).astype(BF16)
    for unit in range(2):
        grads_t[unit] = turned[:, unit * GROUP_LANES : (unit + 1) * GROUP_LANES]

    def place(block, own, far):
        heads[block, :cut] = own[:cut]
        heads[block, cut:FIRST] = far[:cut]
        heads[block, FIRST:second] = own[cut:]
        heads[block, second:WINDOW_ROWS] = far[cut:]

    for block in range(groups):
        heads[block, WINDOW_ROWS:] = jnp.zeros((PADDED_ROWS - WINDOW_ROWS, GROUP_LANES), BF16)
    hidden = hidden_of(far_rows[:, :width], gain, bias)
    for part in range(3):
        weights = w_query[...] if part == 0 else w_key_value[:, slice((part - 1) * width, part * width)]
        far = jnp.dot(hidden, weights, preferred_element_type=F32).astype(BF16)
        for group in range(groups):
            lanes = slice(group * GROUP_LANES, (group + 1) * GROUP_LANES)
            first = part * width + group * GROUP_LANES
            place(part * groups + group, own_heads[:, first : first + GROUP_LANES], far[:, lanes])

    query_t = (query_t0, query_t1)
    counts = (FIRST, SECOND)
    scores, grad_probs, probs, grad_scores = stages[0:2], stages[2:4], stages[4:6], stages[6:8]

    def score(unit, group):
        score_stage(unit, group, groups, counts[unit], heads, grads_t, query_t[unit], scores[unit], grad_probs[unit])

    def softmax(unit):
        softmax_stage(unit, counts[unit], bias_of, scores[unit], grad_probs[unit], probs[unit], grad_scores[unit])

    def product(unit, group):
        product_stage(
            unit, group, groups, counts[unit], heads, grads_t, query_t[unit], probs[unit], grad_scores[unit], results
        )

    probs[1][...] = jnp.zeros_like(probs[1])
    grad_scores[1][...] = jnp.zeros_like(grad_scores[1])
    query_t[1][...] = jnp.zeros_like(query_t[1])
    score(0, 0)

    def body(group, carry):
        product(1, jnp.maximum(group - 1, 0))
        score(1, group)
        softmax(0)
        product(0, group)
        score(0, jnp.minimum(group + 1, groups - 1))
        softmax(1)
        return carry

    lax.fori_loop(0, groups, body, 0, unroll=4)
    product(1, groups - 1)

    def rows_of(first, last):
        return jnp.concatenate(
            [
                jnp.concatenate([results[block, first[0] : first[1]], results[block, last[0] : last[1]]], axis=0)
                for block in range(4 * groups)
            ],
            axis=1,
        )

    own_moves[...] = rows_of((0, cut), (FIRST, second))
    far_moves = rows_of((cut, FIRST), (second, WINDOW_ROWS))
    if kind == "same":
        far_result[...] = far_moves
    else:
        store_tail(far_result, far_rows[...], far_moves, gain, w_query, w_key_value, w_out)


def store_tail(out, rows, moves, gain, w_query, w_key_value, w_out):
    width = rows.shape[1] // 2
    block_output, input_grad = finish(rows[:, :width], rows[:, width:], moves, gain, w_query, w_key_value, w_out)
    out[:, :width] = block_output
    out[:, width:] = input_grad


def tail_kernel(count, *refs):
    rows, moves, weights, out = refs[:count], refs[count : 2 * count], refs[2 * count : -1], refs[-1]
    rows = jnp.concatenate([x[...] for x in rows], axis=0)
    moves = jnp.concatenate([x[...] for x in moves], axis=0)
    store_tail(out, rows, moves, *weights)


SMEM, VMEM, HBM = pltpu.SMEM, pltpu.VMEM, pltpu.HBM


def unpack_kernel(position, table, own, far_same, far_cross, block_output, input_grad, outputs, sems):
    width = block_output.shape[1]
    chunk = width // 2
    token = lax.broadcasted_iota(jnp.int32, (block_output.shape[0], 4 * ROWS), 0)
    one_hot = (token == table[lax.rem(position[0], 2)]).astype(F32).astype(BF16)
    copies = []
    for index in range(4):
        columns = slice(index * chunk, (index + 1) * chunk)
        values = jnp.concatenate([own[:, columns], far_same[:, columns], far_cross[:, columns]], axis=0)
        outputs[index] = picked(one_hot, values)
        target = block_output if index < 2 else input_grad
        copies.append(
            pltpu.make_async_copy(outputs.at[index], target.at[:, pl.ds(index % 2 * chunk, chunk)], sems.at[index])
        )
        copies[-1].start()
    for copy in copies:
        copy.wait()


SMEM, VMEM, HBM = pltpu.SMEM, pltpu.VMEM, pltpu.HBM


def call(kernel, outs, *operands, scratch=(), flops=0, megabytes=24):
    spaces, operands = zip(*operands)
    operands = [pltpu.with_memory_space_constraint(x, HBM) if s == HBM else x for s, x in zip(spaces, operands)]
    outs = [out if len(out) == 3 else (*out, BF16) for out in outs]
    shapes = [jax.ShapeDtypeStruct(shape, kind) for _, shape, kind in outs]
    moved = sum(x.size * x.dtype.itemsize for x in operands) + sum(x.size * 2 for x in shapes)
    return pl.pallas_call(
        kernel,
        out_shape=shapes,
        in_specs=[pl.BlockSpec(memory_space=space) for space in spaces],
        out_specs=[pl.BlockSpec(memory_space=out[0]) for out in outs],
        scratch_shapes=list(scratch),
        compiler_params=pltpu.CompilerParams(vmem_limit_bytes=megabytes << 20),
        cost_estimate=pl.CostEstimate(flops=flops, bytes_accessed=moved, transcendentals=0),
    )(*operands)


def vmem(*arrays):
    return [(VMEM, x) for x in arrays]


def hbm(*arrays):
    return [(HBM, x) for x in arrays]


def like(*arrays):
    return [(VMEM, x.shape, x.dtype) for x in arrays]


def staged(inputs, out_grad, live_rows, live_cols, norm_gain, norm_bias, w_query, w_key_value, w_out):
    token_count, width = inputs.shape
    groups = width // GROUP_LANES
    count = lax.axis_size("seq")
    position = (SMEM, lax.axis_index("seq").reshape(1))
    live = ((SMEM, live_rows), (SMEM, live_cols))
    own_table, send_table = jnp.asarray(OWN_TOKENS[..., None]), jnp.asarray(SEND_TOKENS[..., None])
    unpack_table = jnp.asarray(np.concatenate([OWN_TOKENS, SEND_TOKENS], axis=1)[:, None, :])
    constants = [
        w_query, w_key_value, w_out, norm_gain.reshape(1, width), norm_bias.reshape(1, width),
        jnp.asarray(WINDOW_CODES[..., None]), jnp.asarray(WINDOW_CODES[:, None, :]), unpack_table,
    ]

    pair = [(i, i ^ 1) for i in range(count)]
    across = [(i, (i + 1) % count if i % 2 else (i - 1) % count) for i in range(count)]

    rows_out, heads_out, moves_out = (VMEM, (ROWS, 2 * width)), (VMEM, (ROWS, 3 * width)), (VMEM, (ROWS, 4 * width))
    product = 2 * width * width
    dma = pltpu.SemaphoreType.DMA
    send_same, send_cross, values, grads, own_table = call(
        pack_kernel,
        [rows_out] * 2 + like(inputs, out_grad, own_table),
        position, *hbm(send_table, own_table, inputs, out_grad),
        scratch=[VMEM(send_table.shape, send_table.dtype), dma((4,))],
        flops=4 * ROWS * token_count * 2 * width,
    )
    far_cross_rows = lax.ppermute(send_cross, "seq", across)
    far_same_rows = lax.ppermute(send_same, "seq", pair)
    own_same_rows, own_cross_rows, own_same_heads, own_cross_heads, *rest = call(
        own_kernel,
        [rows_out] * 2 + [heads_out] * 2 + like(*constants),
        position, *vmem(own_table, values, grads), *hbm(*constants),
        scratch=[dma((9,))],
        flops=2 * ROWS * 4 * product,
    )
    w_query, w_key_value, w_out, gain, bias, code_column, code_row, unpack_table = rest
    weights = vmem(w_query, w_key_value, w_out)

    stages = [VMEM((HEADS_PER_GROUP, n, GROUP_LANES), kind) for kind in (F32, F32, BF16, BF16) for n in (FIRST, SECOND)]
    scratch = [
        VMEM((3 * groups, PADDED_ROWS, GROUP_LANES), BF16),
        VMEM((PADDED_ROWS, width), BF16),
        VMEM((2, width, GROUP_LANES), BF16),
        VMEM((4 * groups, PADDED_ROWS, GROUP_LANES), BF16),
        VMEM((2, GROUP_LANES, GROUP_LANES), F32),
        VMEM((GROUP_LANES, GROUP_LANES), BF16),
        VMEM((GROUP_LANES, GROUP_LANES), BF16),
        *stages,
    ]

    def window(kind, own_rows, own_heads, far_rows):
        return call(
            functools.partial(window_kernel, kind), [moves_out if kind == "same" else rows_out, moves_out],
            position, *live, *vmem(code_column, code_row, own_rows, own_heads, far_rows, gain, bias), *weights,
            scratch=scratch, flops=2 * ROWS * 10 * product,
        )

    def tail(rows, moves):
        return call(
            functools.partial(tail_kernel, len(rows)), [(VMEM, (len(rows) * ROWS, 2 * width))],
            *vmem(*rows, *moves, gain), *weights, flops=len(rows) * ROWS * 4 * product,
        )[0]

    far_same_moves, own_same_moves = window("same", own_same_rows, own_same_heads, far_same_rows)
    far_cross, own_cross_moves = window("cross", own_cross_rows, own_cross_heads, far_cross_rows)
    back_cross = lax.ppermute(far_cross, "seq", across)
    far_same = tail([far_same_rows], [far_same_moves])
    back_same = lax.ppermute(far_same, "seq", pair)
    own = tail([own_same_rows, own_cross_rows], [own_same_moves, own_cross_moves])
    return tuple(
        call(
            unpack_kernel, [(HBM, (token_count, width))] * 2, position,
            *vmem(unpack_table, own, back_same, back_cross),
            scratch=[VMEM((4, token_count, width // 2), BF16), dma((4,))],
            flops=8 * ROWS * token_count * 2 * width,
        )
    )


def solution(mesh):
    rows = P(("group", "seq"), None)
    in_specs = (rows, rows, P("group"), P("group"), P(), P(), P(), P(), P())
    return jax.shard_map(staged, mesh=mesh, in_specs=in_specs, out_specs=(rows, rows), check_vma=False)
```

```python
import functools

import jax
import jax.numpy as jnp
import numpy as np
from jax import lax
from jax.experimental import pallas as pl
from jax.experimental.pallas import tpu as pltpu
from jax.sharding import PartitionSpec as P


HEAD_DIM = 32
WT = 8
WH = 7
WW = 7
CELLS = WH * WW
HALF = WT // 2
EPSILON = 1e-05
GROUP_LANES = 128
HEADS_PER_GROUP = GROUP_LANES // HEAD_DIM
SLOTS = (64, 48)
ROWS = sum(SLOTS)
FIRST = 2 * SLOTS[0]
SECOND = 2 * SLOTS[1]
WINDOW_ROWS = FIRST + SECOND
PADDED_ROWS = 2 * GROUP_LANES
MASKED = -1e30
SCALE = HEAD_DIM ** (-0.5)
LOG2E = float(np.log2(np.e))
BF16 = jnp.bfloat16
F32 = jnp.float32
NT = (((1,), (1,)), ((), ()))


def quadrant_cells(quadrant):
    rows = range(WH // 2) if quadrant & 2 else range(WH // 2, WH)
    cols = range(WW // 2) if quadrant & 1 else range(WW // 2, WW)
    return [(row, col) for row in rows for col in cols]


def half_slots(units):
    slots = []
    for quadrant, room in zip(units, SLOTS):
        entries = [(frame, row, col) for frame in range(HALF) for row, col in quadrant_cells(quadrant)]
        slots += entries + [None] * (room - len(entries))
    return slots


def tables():
    takes = {"last": (0, 3), "first": (1, 2)}
    gives = {"last": (1, 2), "first": (0, 3)}

    def tokens(side, units):
        shift = HALF if side == "last" else 0
        return [-1 if s is None else (s[0] + shift) * CELLS + s[1] * WW + s[2] for s in half_slots(units)]

    def codes(slots, second_half):
        return [-1 if s is None else (s[0] + HALF * second_half) * 64 + s[1] * 8 + s[2] for s in slots]

    own, send, window = [], [], []
    for parity in range(2):
        sides = ("last", "first") if parity == 0 else ("first", "last")
        own.append(sum((tokens(side, takes[side]) for side in sides), []))
        send.append(sum((tokens(side, gives[side]) for side in sides), []))
    for side in ("first", "last"):
        slots = half_slots(takes[side])
        mine = codes(slots, side == "first")
        theirs = codes(slots, side == "last")
        cut = SLOTS[0]
        rows = mine[:cut] + theirs[:cut] + mine[cut:] + theirs[cut:]
        window.append(rows + [-1] * (PADDED_ROWS - len(rows)))
    return np.array(own, np.int32), np.array(send, np.int32), np.array(window, np.int32)


OWN_TOKENS, SEND_TOKENS, WINDOW_CODES = tables()


def normalized(values_in):
    values = values_in.astype(F32)
    centred = values - jnp.mean(values, axis=-1, keepdims=True)
    inv_dev = lax.rsqrt(jnp.mean(centred * centred, axis=-1, keepdims=True) + EPSILON)
    return centred * inv_dev, inv_dev


def one_hot_rows(token_column, token_count):
    lanes = lax.broadcasted_iota(jnp.int32, (token_column.shape[0], token_count), 1)
    return (lanes == token_column).astype(F32).astype(BF16)


def picked(one_hot, values):
    return jnp.dot(one_hot, values, preferred_element_type=F32).astype(BF16)


def side_of(kind, position):
    parity = lax.rem(position, 2)
    return 1 - parity if kind == "same" else parity


def pack_kernel(
    position, send_table, own_table, inputs, out_grad, same, cross, values, grads, own_rows, send_rows, sems
):
    width = inputs.shape[1]
    moves = ((send_table, send_rows), (inputs, values), (out_grad, grads), (own_table, own_rows))
    copies = [pltpu.make_async_copy(source, target, sems.at[place]) for place, (source, target) in enumerate(moves)]
    for copy in copies:
        copy.start()
    copies[0].wait()
    one_hot = one_hot_rows(send_rows[lax.rem(position[0], 2)], inputs.shape[0])
    for place, source in enumerate((values, grads)):
        copies[1 + place].wait()
        rows = picked(one_hot, source[...])
        columns = slice(place * width, (place + 1) * width)
        same[:, columns] = rows[:ROWS]
        cross[:, columns] = rows[ROWS:]
    copies[3].wait()


def hidden_of(values, gain, bias):
    unit, _ = normalized(values)
    return (unit * gain[...] + bias[...]).astype(BF16)


def own_kernel(
    position, table, inputs, out_grad, w_query, w_key_value, w_out, gain, bias, code_column, code_row, unpack_table,
    rows_same, rows_cross, heads_same, heads_cross, query_copy, pair_copy, out_copy, gain_copy, bias_copy,
    column_copy, row_copy, unpack_copy, sems,
):
    width = inputs.shape[1]
    halves = [pl.ds(part * width, width) for part in range(2)]
    moves = [(gain, gain_copy), (bias, bias_copy), (w_query, query_copy)]
    moves += [(w_key_value.at[:, part], pair_copy.at[:, part]) for part in halves]
    moves += [(w_out, out_copy), (code_column, column_copy), (code_row, row_copy), (unpack_table, unpack_copy)]
    copies = [pltpu.make_async_copy(source, target, sems.at[place]) for place, (source, target) in enumerate(moves)]
    for copy in copies:
        copy.start()
    one_hot = one_hot_rows(table[lax.rem(position[0], 2)], inputs.shape[0])
    values = picked(one_hot, inputs[...])
    copies[0].wait()
    copies[1].wait()
    hidden = hidden_of(values, gain_copy, bias_copy)
    grads = picked(one_hot, out_grad[...])
    for place, rows in enumerate((values, grads)):
        columns = slice(place * width, (place + 1) * width)
        rows_same[:, columns] = rows[:ROWS]
        rows_cross[:, columns] = rows[ROWS:]
    for part in range(3):
        copies[2 + part].wait()
        weights = query_copy[...] if part == 0 else pair_copy[:, halves[part - 1]]
        result = jnp.dot(hidden, weights, preferred_element_type=F32).astype(BF16)
        columns = slice(part * width, (part + 1) * width)
        heads_same[:, columns] = result[:ROWS]
        heads_cross[:, columns] = result[ROWS:]
    for copy in copies[5:]:
        copy.wait()


def cell_codes(slots, place, frames):
    frame = slots >> 6
    word = jnp.zeros_like(slots)
    for index, frame_word in enumerate(frames):
        word = jnp.where(frame == index, frame_word, word)
    row, col = (slots >> 3) & 7, slots & 7
    live = (slots >= 0) & (row < (word >> 8)) & (col < ((word >> 4) & 15))
    return jnp.where(live, word & 1, -1 - place)


def head_rows(h):
    return slice(h * HEAD_DIM, (h + 1) * HEAD_DIM)


def head_lanes(h):
    return slice(h * GROUP_LANES, (h + 1) * GROUP_LANES)


def block_diagonal(values):
    zero = jnp.zeros((HEAD_DIM, GROUP_LANES), values.dtype)
    return jnp.concatenate(
        [
            jnp.concatenate([values[head_rows(r)] if r == h else zero for r in range(HEADS_PER_GROUP)], axis=0)
            for h in range(HEADS_PER_GROUP)
        ],
        axis=1,
    )


def score_stage(unit, group, groups, count, heads, grads_t, query_t, scores, grad_probs):
    base = unit * GROUP_LANES
    keys = slice(base, base + count)
    query = heads[group, base : base + GROUP_LANES].T
    query_t[...] = query
    grad = grads_t[unit, pl.ds(pl.multiple_of(group * GROUP_LANES, GROUP_LANES), GROUP_LANES)]
    score = jnp.dot(heads[groups + group, keys], block_diagonal(query), preferred_element_type=F32)
    grad_prob = jnp.dot(heads[2 * groups + group, keys], block_diagonal(grad), preferred_element_type=F32)
    for h in range(HEADS_PER_GROUP):
        scores[h] = score[:, head_lanes(h)]
        grad_probs[h] = grad_prob[:, head_lanes(h)]


def softmax_stage(unit, count, bias_of, scores, grad_probs, probs, grad_scores):
    for h in range(HEADS_PER_GROUP):
        score = scores[h] * (SCALE * LOG2E) + bias_of[unit, :count]
        raw = jnp.exp2(score - jnp.max(score, axis=0, keepdims=True))
        inverse = 1.0 / jnp.sum(raw, axis=0, keepdims=True)
        grad_prob = grad_probs[h]
        row_dot = jnp.sum(raw * grad_prob, axis=0, keepdims=True) * inverse
        probs[h] = (raw * inverse).astype(BF16)
        grad_scores[h] = (raw * ((grad_prob - row_dot) * (inverse * SCALE))).astype(BF16)


def product_stage(unit, group, groups, count, heads, grads_t, query_t, probs, grad_scores, results):
    base = unit * GROUP_LANES
    keys = slice(base, base + count)
    grad = grads_t[unit, pl.ds(pl.multiple_of(group * GROUP_LANES, GROUP_LANES), GROUP_LANES)]
    key_t, value_t = heads[groups + group, keys].T, heads[2 * groups + group, keys].T

    def per_key(left, right):
        left = jnp.concatenate([left[h] for h in range(HEADS_PER_GROUP)], axis=1)
        return lax.dot_general(left, block_diagonal(right), NT, preferred_element_type=F32).astype(BF16)

    def per_query(left, right):
        parts = [jnp.dot(left[head_rows(h)], right[h], preferred_element_type=F32) for h in range(HEADS_PER_GROUP)]
        return jnp.concatenate(parts, axis=0).T[:count].astype(BF16)

    results[group, keys] = per_query(value_t, probs)
    results[groups + group, keys] = per_query(key_t, grad_scores)
    results[2 * groups + group, keys] = per_key(grad_scores, query_t[...])
    results[3 * groups + group, keys] = per_key(probs, grad)


def output_of(rows, context, w_out):
    width = context.shape[1]
    context_out = jnp.dot(context, w_out[...], preferred_element_type=F32)
    return (rows[:, :width].astype(F32) + context_out).astype(BF16)


def input_grad_of(rows, moves, gain, w_query, w_key_value):
    count, width = rows.shape[0], rows.shape[1] // 2
    fill = -count % GROUP_LANES
    if fill:
        moves = jnp.concatenate([moves, jnp.zeros((fill, 3 * width), BF16)], axis=0)
    grad_hidden = lax.dot_general(w_query[...], moves[:, :width], NT, preferred_element_type=F32)
    grad_hidden = grad_hidden + lax.dot_general(w_key_value[...], moves[:, width:], NT, preferred_element_type=F32)
    grad_hidden = grad_hidden.T[:count]
    unit, inv_dev = normalized(rows[:, :width])
    scaled = grad_hidden * gain[...]
    centred = scaled - jnp.mean(scaled, axis=-1, keepdims=True)
    norm_grad = inv_dev * (centred - unit * jnp.mean(scaled * unit, axis=-1, keepdims=True))
    return (rows[:, width:].astype(F32) + norm_grad).astype(BF16)


def window_kernel(
    kind, position, live_rows, live_cols, code_column, code_row, own_rows, own_heads, far_rows,
    gain, bias, w_query, w_key_value, w_out, own_moves, far_moves, *rest,
):
    far_output, rest = (rest[:1], rest[1:]) if kind == "cross" else ((), rest)
    heads, window_grads, grads_t, results, bias_of, query_t0, query_t1, *stages = rest
    width = far_rows.shape[1] // 2
    groups = width // GROUP_LANES
    cut, second = SLOTS[0], FIRST + SLOTS[1]
    side = side_of(kind, position[0])
    total = live_rows.shape[0]
    frames = []
    for index in range(WT):
        frame = lax.rem(position[0] * WT + (side * 2 - 1) * HALF + index + total, total)
        frames.append(live_rows[frame] * 256 + live_cols[frame] * 16 + (frame < HALF).astype(jnp.int32))
    by_key = cell_codes(code_column[side], lax.broadcasted_iota(jnp.int32, (PADDED_ROWS, 1), 0), frames)
    by_query = cell_codes(code_row[side], lax.broadcasted_iota(jnp.int32, (1, PADDED_ROWS), 1), frames)
    for unit in range(2):
        block = slice(unit * GROUP_LANES, (unit + 1) * GROUP_LANES)
        bias_of[unit] = jnp.where(by_key[block] == by_query[:, block], 0.0, MASKED)

    window_grads[:cut] = own_rows[:cut, width:]
    window_grads[cut:FIRST] = far_rows[:cut, width:]
    window_grads[FIRST:second] = own_rows[cut:, width:]
    window_grads[second:WINDOW_ROWS] = far_rows[cut:, width:]
    window_grads[WINDOW_ROWS:] = jnp.zeros((PADDED_ROWS - WINDOW_ROWS, width), BF16)
    turned = lax.dot_general(w_out[...], window_grads[...], NT, preferred_element_type=F32).astype(BF16)
    for unit in range(2):
        grads_t[unit] = turned[:, unit * GROUP_LANES : (unit + 1) * GROUP_LANES]

    def place(block, own, far):
        heads[block, :cut] = own[:cut]
        heads[block, cut:FIRST] = far[:cut]
        heads[block, FIRST:second] = own[cut:]
        heads[block, second:WINDOW_ROWS] = far[cut:]

    for block in range(groups):
        heads[block, WINDOW_ROWS:] = jnp.zeros((PADDED_ROWS - WINDOW_ROWS, GROUP_LANES), BF16)
    hidden = hidden_of(far_rows[:, :width], gain, bias)
    for part in range(3):
        weights = w_query[...] if part == 0 else w_key_value[:, slice((part - 1) * width, part * width)]
        far = jnp.dot(hidden, weights, preferred_element_type=F32).astype(BF16)
        for group in range(groups):
            lanes = slice(group * GROUP_LANES, (group + 1) * GROUP_LANES)
            first = part * width + group * GROUP_LANES
            place(part * groups + group, own_heads[:, first : first + GROUP_LANES], far[:, lanes])

    query_t = (query_t0, query_t1)
    counts = (FIRST, SECOND)
    scores, grad_probs, probs, grad_scores = stages[0:2], stages[2:4], stages[4:6], stages[6:8]

    def score(unit, group):
        score_stage(unit, group, groups, counts[unit], heads, grads_t, query_t[unit], scores[unit], grad_probs[unit])

    def softmax(unit):
        softmax_stage(unit, counts[unit], bias_of, scores[unit], grad_probs[unit], probs[unit], grad_scores[unit])

    def product(unit, group):
        product_stage(
            unit, group, groups, counts[unit], heads, grads_t, query_t[unit], probs[unit], grad_scores[unit], results
        )

    probs[1][...] = jnp.zeros_like(probs[1])
    grad_scores[1][...] = jnp.zeros_like(grad_scores[1])
    query_t[1][...] = jnp.zeros_like(query_t[1])
    score(0, 0)

    def body(group, carry):
        product(1, jnp.maximum(group - 1, 0))
        score(1, group)
        softmax(0)
        product(0, group)
        score(0, jnp.minimum(group + 1, groups - 1))
        softmax(1)
        return carry

    lax.fori_loop(0, groups, body, 0, unroll=4)
    product(1, groups - 1)

    def rows_of(first, last):
        return jnp.concatenate(
            [
                jnp.concatenate([results[block, first[0] : first[1]], results[block, last[0] : last[1]]], axis=0)
                for block in range(4 * groups)
            ],
            axis=1,
        )

    own_moves[...] = rows_of((0, cut), (FIRST, second))
    far_moved = rows_of((cut, FIRST), (second, WINDOW_ROWS))
    if kind == "same":
        far_moves[...] = far_moved
    else:
        far_moves[...] = far_moved[:, width:]
        far_output[0][...] = output_of(far_rows[...], far_moved[:, :width], w_out)


def far_tail_kernel(rows_same, rows_cross, moves_same, moves_cross, gain, w_query, w_key_value, w_out, same, cross):
    width = cross.shape[1]
    rows = jnp.concatenate([rows_same[...], rows_cross[...]], axis=0)
    moves = jnp.concatenate([moves_same[:, width:], moves_cross[...]], axis=0)
    input_grad = input_grad_of(rows, moves, gain, w_query, w_key_value)
    cross[...] = input_grad[ROWS:]
    same[:, width:] = input_grad[:ROWS]
    same[:, :width] = output_of(rows_same[...], moves_same[:, :width], w_out)


def own_tail_kernel(rows_same, rows_cross, moves_same, moves_cross, gain, w_query, w_key_value, w_out, out):
    width = out.shape[1] // 2
    rows = jnp.concatenate([rows_same[...], rows_cross[...]], axis=0)
    moves = jnp.concatenate([moves_same[...], moves_cross[...]], axis=0)
    out[:, :width] = output_of(rows, moves[:, :width], w_out)
    out[:, width:] = input_grad_of(rows, moves[:, width:], gain, w_query, w_key_value)


SMEM, VMEM, HBM = pltpu.SMEM, pltpu.VMEM, pltpu.HBM


def unpack_kernel(
    position, table, own, far_same, far_output, far_grad, block_output, input_grad, outputs, sems
):
    width = block_output.shape[1]
    chunk = width // 2
    token = lax.broadcasted_iota(jnp.int32, (block_output.shape[0], 4 * ROWS), 0)
    one_hot = (token == table[lax.rem(position[0], 2)]).astype(F32).astype(BF16)
    copies = []
    for index in range(4):
        columns = slice(index * chunk, (index + 1) * chunk)
        far_cross = far_output if index < 2 else far_grad
        place = pl.ds(index % 2 * chunk, chunk)
        values = jnp.concatenate([own[:, columns], far_same[:, columns], far_cross[:, place]], axis=0)
        outputs[index] = picked(one_hot, values)
        target = block_output if index < 2 else input_grad
        copies.append(
            pltpu.make_async_copy(outputs.at[index], target.at[:, place], sems.at[index])
        )
        copies[-1].start()
    for copy in copies:
        copy.wait()


SMEM, VMEM, HBM = pltpu.SMEM, pltpu.VMEM, pltpu.HBM


def call(kernel, outs, *operands, scratch=(), flops=0, megabytes=24):
    spaces, operands = zip(*operands)
    operands = [pltpu.with_memory_space_constraint(x, HBM) if s == HBM else x for s, x in zip(spaces, operands)]
    outs = [out if len(out) == 3 else (*out, BF16) for out in outs]
    shapes = [jax.ShapeDtypeStruct(shape, kind) for _, shape, kind in outs]
    moved = sum(x.size * x.dtype.itemsize for x in operands) + sum(x.size * 2 for x in shapes)
    return pl.pallas_call(
        kernel,
        out_shape=shapes,
        in_specs=[pl.BlockSpec(memory_space=space) for space in spaces],
        out_specs=[pl.BlockSpec(memory_space=out[0]) for out in outs],
        scratch_shapes=list(scratch),
        compiler_params=pltpu.CompilerParams(vmem_limit_bytes=megabytes << 20),
        cost_estimate=pl.CostEstimate(flops=flops, bytes_accessed=moved, transcendentals=0),
    )(*operands)


def vmem(*arrays):
    return [(VMEM, x) for x in arrays]


def hbm(*arrays):
    return [(HBM, x) for x in arrays]


def like(*arrays):
    return [(VMEM, x.shape, x.dtype) for x in arrays]


def staged(inputs, out_grad, live_rows, live_cols, norm_gain, norm_bias, w_query, w_key_value, w_out):
    token_count, width = inputs.shape
    groups = width // GROUP_LANES
    count = lax.axis_size("seq")
    position = (SMEM, lax.axis_index("seq").reshape(1))
    live = ((SMEM, live_rows), (SMEM, live_cols))
    own_table, send_table = jnp.asarray(OWN_TOKENS[..., None]), jnp.asarray(SEND_TOKENS[..., None])
    unpack_table = jnp.asarray(np.concatenate([OWN_TOKENS, SEND_TOKENS], axis=1)[:, None, :])
    constants = [
        w_query, w_key_value, w_out, norm_gain.reshape(1, width), norm_bias.reshape(1, width),
        jnp.asarray(WINDOW_CODES[..., None]), jnp.asarray(WINDOW_CODES[:, None, :]), unpack_table,
    ]

    pair = [(i, i ^ 1) for i in range(count)]
    across = [(i, (i + 1) % count if i % 2 else (i - 1) % count) for i in range(count)]

    rows_out, heads_out, moves_out = (VMEM, (ROWS, 2 * width)), (VMEM, (ROWS, 3 * width)), (VMEM, (ROWS, 4 * width))
    product = 2 * width * width
    dma = pltpu.SemaphoreType.DMA
    send_same, send_cross, values, grads, own_table = call(
        pack_kernel,
        [rows_out] * 2 + like(inputs, out_grad, own_table),
        position, *hbm(send_table, own_table, inputs, out_grad),
        scratch=[VMEM(send_table.shape, send_table.dtype), dma((4,))],
        flops=4 * ROWS * token_count * 2 * width,
    )
    far_cross_rows = lax.ppermute(send_cross, "seq", across)
    far_same_rows = lax.ppermute(send_same, "seq", pair)
    own_same_rows, own_cross_rows, own_same_heads, own_cross_heads, *rest = call(
        own_kernel,
        [rows_out] * 2 + [heads_out] * 2 + like(*constants),
        position, *vmem(own_table, values, grads), *hbm(*constants),
        scratch=[dma((9,))],
        flops=2 * ROWS * 4 * product,
    )
    w_query, w_key_value, w_out, gain, bias, code_column, code_row, unpack_table = rest
    weights = vmem(w_query, w_key_value, w_out)

    stages = [VMEM((HEADS_PER_GROUP, n, GROUP_LANES), kind) for kind in (F32, F32, BF16, BF16) for n in (FIRST, SECOND)]
    scratch = [
        VMEM((3 * groups, PADDED_ROWS, GROUP_LANES), BF16),
        VMEM((PADDED_ROWS, width), BF16),
        VMEM((2, width, GROUP_LANES), BF16),
        VMEM((4 * groups, PADDED_ROWS, GROUP_LANES), BF16),
        VMEM((2, GROUP_LANES, GROUP_LANES), F32),
        VMEM((GROUP_LANES, GROUP_LANES), BF16),
        VMEM((GROUP_LANES, GROUP_LANES), BF16),
        *stages,
    ]

    half_out = (VMEM, (ROWS, width))

    def window(kind, own_rows, own_heads, far_rows):
        return call(
            functools.partial(window_kernel, kind),
            [moves_out] * 2 if kind == "same" else [moves_out, heads_out, half_out],
            position, *live, *vmem(code_column, code_row, own_rows, own_heads, far_rows, gain, bias), *weights,
            scratch=scratch, flops=2 * ROWS * 8 * product,
        )

    own_same_moves, far_same_moves = window("same", own_same_rows, own_same_heads, far_same_rows)
    own_cross_moves, far_cross_moves, far_output = window("cross", own_cross_rows, own_cross_heads, far_cross_rows)
    back_output = lax.ppermute(far_output, "seq", across)
    far_same, far_grad = call(
        far_tail_kernel, [rows_out, half_out],
        *vmem(far_same_rows, far_cross_rows, far_same_moves, far_cross_moves, gain), *weights,
        flops=2 * ROWS * 4 * product,
    )
    back_grad = lax.ppermute(far_grad, "seq", across)
    back_same = lax.ppermute(far_same, "seq", pair)
    (own,) = call(
        own_tail_kernel, [(VMEM, (2 * ROWS, 2 * width))],
        *vmem(own_same_rows, own_cross_rows, own_same_moves, own_cross_moves, gain), *weights,
        flops=2 * ROWS * 4 * product,
    )
    return tuple(
        call(
            unpack_kernel, [(HBM, (token_count, width))] * 2, position,
            *vmem(unpack_table, own, back_same, back_output, back_grad),
            scratch=[VMEM((4, token_count, width // 2), BF16), dma((4,))],
            flops=8 * ROWS * token_count * 2 * width,
        )
    )


def solution(mesh):
    rows = P(("group", "seq"), None)
    in_specs = (rows, rows, P("group"), P("group"), P(), P(), P(), P(), P())
    return jax.shard_map(staged, mesh=mesh, in_specs=in_specs, out_specs=(rows, rows), check_vma=False)
```
